256 devices in a mesh: dp: 4 (over y), ctx: 64 (over z, x, core).
Axes of the slice: x: 4, y: 4, z: 8, core: 2. Of those that a mesh axis runs over, the one named last changes fastest.
Arguments:
- gate_in: bfloat16 [4, 8192, 2048], P('dp', 'ctx'), may hold values from -6 to 6
- key_in: bfloat16 [4, 8192, 2048], P('dp', 'ctx'), may hold values from -6 to 6
- value_in: bfloat16 [4, 8192, 2048], P('dp', 'ctx'), may hold values from -6 to 6
- cotangent: bfloat16 [4, 8192, 2048], P('dp', 'ctx'), may hold values from -6 to 6
- doc_starts: int32 [4, 17], P('dp'), may hold values from 0 to 7936, as said below
- filters: bfloat16 [128, 128], replicated, may hold values from -0.5 to 0.5
Outputs:
- output: bfloat16 [4, 8192, 2048], P('dp', 'ctx')
- grad_query: bfloat16 [4, 8192, 2048], P('dp', 'ctx')
- grad_key: bfloat16 [4, 8192, 2048], P('dp', 'ctx')
- grad_value: bfloat16 [4, 8192, 2048], P('dp', 'ctx')
- filter_grad: float32 [128, 128], replicated
The draws below stay inside these ranges and needn't reach their ends.
Inputs may be any that keep to these rules, and one draw needn't show every extreme that they name: `doc_starts`: each row holds 17 strictly rising multiples of 128; the first is 0 and the last is 7936.
All inputs are finite; a program needn't handle non-finite values.
Results may differ from the reference program's by a relative error of at most 0.0049.
Values may be sent and summed in bfloat16 or wider, within the bound.
A program may use at most 192 MiB of HBM per device.

```python
import jax
import jax.numpy as jnp
from jax import lax

D = 2048
TAPS = 128
ROWS_DEV = 128
FILTERS = 128
SEQ = 8192
DOCS = 17
N_DP = 4
N_CTX = 64


def draw_doc_starts(key, part):
    tile_total = SEQ // TAPS
    per_device = ROWS_DEV // TAPS
    tile_ids = jnp.arange(tile_total, dtype=jnp.int32)
    allowed = (tile_ids >= 2) & (tile_ids <= tile_total - 3)
    allowed = allowed & (tile_ids != per_device * (N_CTX // 2))
    allowed = allowed & (tile_ids != per_device * (N_CTX // 2 + 1))

    def one_row(index):
        subkey = jax.random.fold_in(key, index)
        ranks = jax.random.permutation(subkey, tile_total).astype(jnp.int32) + 1
        scores = jnp.where(allowed, ranks, 0).astype(jnp.int32)
        picked = lax.top_k(scores, DOCS - 2)[1].astype(jnp.int32)
        inner = jnp.sort(picked)
        head = jnp.zeros((1,), jnp.int32)
        tail = jnp.full((1,), tile_total - 2, jnp.int32)
        return jnp.concatenate([head, inner, tail]) * TAPS
    return jax.vmap(one_row)(jnp.arange(N_DP, dtype=jnp.int32)).astype(jnp.int32)


def block_levels(key, dims, cuts, low, top_value):
    def one(position, blocks):
        draws = jax.random.uniform(jax.random.fold_in(jax.random.fold_in(key, 6), position), (blocks,), jnp.float32, low / len(cuts), top_value / len(cuts))
        return jnp.repeat(jnp.exp(draws), dims[position] // blocks).reshape((-1,) + (1,) * (len(dims) - position - 1))

    factor_of = one(*cuts[0])
    for cut in cuts[1:]:
        factor_of = factor_of * one(*cut)
    return factor_of


def centred(rng, extent, scale, most, split=(), held_as=jnp.bfloat16):
    values = jax.random.normal(rng, extent, jnp.float32) * scale
    if len(split) > 0:
        values = block_levels(rng, extent, split, -0.22, 0.18) * values
    return jnp.clip(values, min=-most, max=most).astype(held_as)


def setup_inputs(seed: int = 0) -> dict:
    arg_keys = jax.random.split(jax.random.key(seed), 7)
    gate_in = centred(arg_keys[0], (N_DP, SEQ, D), 1.0, 6.0, ((0, 4), (1, 64)))
    key_in = centred(arg_keys[1], (N_DP, SEQ, D), 1.0, 6.0, ((0, 4), (1, 64)))
    value_in = centred(arg_keys[2], (N_DP, SEQ, D), 1.0, 6.0, ((0, 4), (1, 64)))
    cotangent = centred(arg_keys[3], (N_DP, SEQ, D), 1.0, 6.0, ((0, 4), (1, 64)))
    doc_starts = draw_doc_starts(jax.random.fold_in(arg_keys[6], 71), 0)
    filters = centred(arg_keys[5], (FILTERS, TAPS), TAPS ** -0.5, 0.5)
    return dict(gate_in=gate_in, key_in=key_in, value_in=value_in, cotangent=cotangent, doc_starts=doc_starts, filters=filters)


def build_tiles(filters):
    group_count = filters.shape[0]
    tap_count = filters.shape[1]
    zero_block = jnp.zeros((group_count, tap_count), filters.dtype)
    diag_line = jnp.concatenate([zero_block, filters[:, ::-1], zero_block], axis=1)
    flattened = jnp.tile(diag_line, (1, tap_count))
    stride = 3 * tap_count - 1
    flattened = flattened[:, tap_count - 1: tap_count - 1 + tap_count * stride]
    return flattened.reshape(group_count, tap_count, stride)[:, :, :2 * tap_count]


def diagonal_sums(tile_grads):
    group_count = tile_grads.shape[0]
    tap_count = tile_grads.shape[1]
    stride = 3 * tap_count - 1
    padded = jnp.pad(tile_grads, ((0, 0), (0, 0), (0, stride - 2 * tap_count)))
    flattened = padded.reshape(group_count, tap_count * stride)
    flattened = jnp.pad(flattened, ((0, 0), (tap_count - 1, 1)))
    diag_line = jnp.sum(flattened.reshape(group_count, tap_count, 3 * tap_count), axis=1)
    return diag_line[:, tap_count:2 * tap_count][:, ::-1]


def keep_mask(starts_row, first_block, block_total, tap_count):
    block_ids = first_block + jnp.arange(block_total, dtype=jnp.int32)
    is_start = jnp.any(starts_row[None, :] == block_ids[:, None] * tap_count, axis=1)
    return jnp.where(is_start, 0.0, 1.0).astype(jnp.float32)


def reference(gate_in, key_in, value_in, cotangent, doc_starts, filters):
    toeplitz = build_tiles(filters).astype(jnp.float32)
    tap_count = filters.shape[1]
    group_count = filters.shape[0]
    channels = gate_in.shape[2]
    group_width = channels // group_count
    seq_len = gate_in.shape[1]
    block_count = seq_len // tap_count
    highest = lax.Precision.HIGHEST

    def one_sequence(packed):
        gate_local, key_local, value_local, upstream, starts_row = packed
        keep_vals = keep_mask(starts_row, 0, block_count, tap_count)
        product = (key_local.astype(jnp.float32) * value_local.astype(jnp.float32)).astype(jnp.bfloat16)
        shaped = product.reshape(block_count, tap_count, group_count, group_width)
        earlier = jnp.concatenate([jnp.zeros((1, tap_count, group_count, group_width), jnp.bfloat16), shaped[:-1]], axis=0)
        earlier = earlier * keep_vals[:, None, None, None].astype(jnp.bfloat16)
        window = jnp.concatenate([earlier, shaped], axis=1).astype(jnp.float32)
        conv_out = jnp.einsum("ftj,bjfc->btfc", toeplitz, window, precision=highest).reshape(seq_len, channels)
        gated = (gate_local.astype(jnp.float32) * conv_out).astype(jnp.bfloat16)
        grad_query = (upstream.astype(jnp.float32) * conv_out).astype(jnp.bfloat16)
        grad_conv = (upstream.astype(jnp.float32) * gate_local.astype(jnp.float32)).astype(jnp.bfloat16)
        grad_blocks = grad_conv.reshape(block_count, tap_count, group_count, group_width).astype(jnp.float32)
        spread = jnp.einsum("ftj,btfc->bjfc", toeplitz, grad_blocks, precision=highest)
        current = spread[:, tap_count:]
        carried = spread[:, :tap_count] * keep_vals[:, None, None, None]
        following = jnp.concatenate([carried[1:], jnp.zeros((1, tap_count, group_count, group_width), jnp.float32)], axis=0)
        grad_mixed = (current + following).reshape(seq_len, channels)
        grad_key = (grad_mixed * value_local.astype(jnp.float32)).astype(jnp.bfloat16)
        grad_value = (grad_mixed * key_local.astype(jnp.float32)).astype(jnp.bfloat16)
        tile_grads = jnp.einsum("btfc,bjfc->ftj", grad_blocks, window, precision=highest)
        return gated, grad_query, grad_key, grad_value, tile_grads

    results = lax.map(one_sequence, (gate_in, key_in, value_in, cotangent, doc_starts))
    filter_grad = diagonal_sums(jnp.sum(results[4], axis=0))
    return (results[0], results[1], results[2], results[3], filter_grad)
```

```python
import functools

import jax
import jax.numpy as jnp
from jax import lax
from jax.experimental import pallas as pl
from jax.experimental.pallas import tpu as pltpu
from jax.sharding import PartitionSpec as P

F32, BF16 = jnp.float32, jnp.bfloat16
MESH = pl.DeviceIdType.MESH
NT = (((1,), (1,)), ((), ()))


def build_bases(h_ref, hs_ref, b1_ref, b2_ref):
    lane = lax.broadcasted_iota(jnp.int32, (128, 128), 1)
    sub = lax.broadcasted_iota(jnp.int32, (128, 128), 0)
    flip = (lane + sub == 127).astype(BF16)
    h = h_ref[...]
    hs_ref[0] = h.astype(F32)
    hs_ref[1] = jnp.dot(h, flip, preferred_element_type=F32)
    r = lax.broadcasted_iota(jnp.int32, (16, 128), 0)
    m = lax.broadcasted_iota(jnp.int32, (16, 128), 1)

    def step(i, _):
        for j in range(8):
            f = i * 8 + j
            rows = pl.ds(pl.multiple_of(f * 16, 16), 16)
            fwd = jnp.broadcast_to(hs_ref[0, pl.ds(f, 1), :], (16, 128))
            rev = jnp.broadcast_to(hs_ref[1, pl.ds(f, 1), :], (16, 128))
            fwd = pltpu.roll(fwd, 0, 1, stride=1, stride_axis=0)
            rev = pltpu.roll(rev, 1, 1, stride=1, stride_axis=0)
            b2_ref[rows, 0:128] = jnp.where(m >= r, fwd, 0.0).astype(BF16)
            b2_ref[rows, 128:256] = jnp.where(m < r, fwd, 0.0).astype(BF16)
            b1_ref[rows, 0:128] = jnp.where(m >= r + 1, rev, 0.0).astype(BF16)
            b1_ref[rows, 128:256] = jnp.where(m < r + 1, rev, 0.0).astype(BF16)
        return 0

    lax.fori_loop(0, 16, step, 0)


def pick(full, half, group):
    lanes = slice(128 * half, 128 * half + 128)
    out = full[112:128, lanes]
    for g in range(6, -1, -1):
        out = jnp.where(group == g, full[16 * g : 16 * g + 16, lanes], out)
    return out


def slab(ref, a, blk):
    return jnp.concatenate(
        [ref[16 * a : 16 * a + 144, blk], ref[16 * a + 16 : 16 * a + 160, blk]], axis=1
    )


def block_of(i):
    return pl.ds(pl.multiple_of(i * 128, 128), 128)


def lane_group():
    return lax.broadcasted_iota(jnp.int32, (16, 128), 1) // 16


def conv_block(i, q_ref, k_ref, v_ref, c_ref, u_ref, d_ref, b1_ref, b2_ref, outs):
    z_ref, gq_ref, gk_ref, gv_ref = outs
    blk = block_of(i)
    group = lane_group()
    lhs1 = b1_ref[blk, 0:144]
    lhs2 = b2_ref[blk, 0:144]
    for a in range(0, 8, 2):
        y = jnp.dot(lhs1, slab(u_ref, a, blk), preferred_element_type=F32)
        du = jnp.dot(lhs2, slab(d_ref, a, blk), preferred_element_type=F32)
        for half in range(2):
            rows = slice(16 * (a + half), 16 * (a + half) + 16)
            yv = pick(y, half, group)
            z_ref[rows, blk] = (q_ref[rows, blk].astype(F32) * yv).astype(BF16)
            gq_ref[rows, blk] = (c_ref[rows, blk].astype(F32) * yv).astype(BF16)
            dv = pick(du, half, group)
            gk_ref[rows, blk] = (v_ref[rows, blk].astype(F32) * dv).astype(BF16)
            gv_ref[rows, blk] = (k_ref[rows, blk].astype(F32) * dv).astype(BF16)


def pair_sums(i, u_ref, d_ref, g_ref):
    blk = block_of(i)
    group = lane_group()
    total = jnp.zeros((128, 144), F32)
    for a in range(0, 8, 2):
        pair = []
        for half in range(2):
            start = 128 + 16 * (a + half)
            rows = u_ref[start : start + 16, blk]
            spread = [jnp.where(group == g, rows, jnp.zeros_like(rows)) for g in range(8)]
            pair.append(jnp.concatenate(spread, axis=0))
        total = total + lax.dot_general(
            jnp.concatenate(pair, axis=1), slab(d_ref, a, blk), NT, preferred_element_type=F32
        )
    g_ref[blk, 0:144] = total


def diagonals(i, g_ref):
    rows = block_of(i)
    lane = lax.broadcasted_iota(jnp.int32, (128, 128), 1)
    r = lax.broadcasted_iota(jnp.int32, (128, 128), 0) % 16
    both = jnp.where(lane < r, g_ref[rows, 128:256], g_ref[rows, 0:128])
    parts = [
        both[16 * f : 16 * f + 8] + pltpu.roll(both[16 * f + 8 : 16 * f + 16], 120, 1)
        for f in range(8)
    ]
    sub = lax.broadcasted_iota(jnp.int32, (8, 128), 0)
    for step in (4, 2, 1):
        low = sub % (2 * step) < step
        merged = []
        for f in range(step):
            one, two = parts[f], parts[f + step]
            first = jnp.where(low, one, pltpu.roll(two, step, 0))
            second = jnp.where(low, pltpu.roll(one, 8 - step, 0), two)
            merged.append(first + pltpu.roll(second, 128 - step, 1))
        parts = merged
    return parts[0]


def tile_kernel(h_ref, q_ref, k_ref, v_ref, c_ref, up_ref, dn_ref,
                z_ref, gq_ref, gk_ref, gv_ref, fg_ref,
                u_ref, d_ref, b1_ref, b2_ref, hs_ref, g_ref):
    build_bases(h_ref, hs_ref, b1_ref, b2_ref)
    u_ref[0:128] = up_ref[...]
    d_ref[128:256] = dn_ref[...]
    u_ref[128:256] = (k_ref[...].astype(F32) * v_ref[...].astype(F32)).astype(BF16)
    d_ref[0:128] = (c_ref[...].astype(F32) * q_ref[...].astype(F32)).astype(BF16)
    outs = (z_ref, gq_ref, gk_ref, gv_ref)

    def step(i, _):
        pair_sums(i, u_ref, d_ref, g_ref)
        conv_block(i, q_ref, k_ref, v_ref, c_ref, u_ref, d_ref, b1_ref, b2_ref, outs)
        return 0

    lax.fori_loop(0, 16, step, 0)

    def last(i, _):
        for j in range(4):
            rows = diagonals(4 * i + j, g_ref)
            fg_ref[8 * i + 2 * j] = rows[0:4]
            fg_ref[8 * i + 2 * j + 1] = rows[4:8]
        return 0

    lax.fori_loop(0, 4, last, 0)


def tile_ops(h, q, k, v, c, up, dn):
    sd = jax.ShapeDtypeStruct
    vmem = pl.BlockSpec(memory_space=pltpu.VMEM)
    return pl.pallas_call(
        tile_kernel,
        out_shape=[sd((128, 2048), BF16)] * 4 + [sd((32, 4, 128), F32)],
        in_specs=[vmem] * 7,
        out_specs=[vmem] * 5,
        scratch_shapes=[pltpu.VMEM((256, 2048), BF16)] * 2
        + [pltpu.VMEM((2048, 256), BF16)] * 2
        + [pltpu.VMEM((2, 128, 128), F32), pltpu.VMEM((2048, 256), F32)],
        name="tile_ops",
    )(h, q, k, v, c, up, dn)


def reduce_everywhere(fg_ref, put_ref, rs_buf, z_buf, part, sems):
    rs_send, rs_recv, z_send, z_recv, ag_send, ag_recv = sems
    ctx = lax.axis_index("ctx")
    own = lax.axis_index("dp") * 8 + lax.rem(ctx, 8)
    z = ctx // 8

    def plane(k):
        p = lax.rem(own + k, 32)
        return p, {"dp": p // 8, "ctx": z * 8 + lax.rem(p, 8)}

    def along(k):
        p = lax.rem(z + k, 8)
        return p, {"ctx": p * 8 + lax.rem(ctx, 8)}

    def rs(k):
        p, where = plane(k)
        return p, pltpu.make_async_remote_copy(
            fg_ref.at[p], rs_buf.at[own], rs_send.at[k], rs_recv.at[own], where, MESH)

    def rs_in(k):
        p, where = plane(k)
        return pltpu.make_async_remote_copy(
            fg_ref.at[p], rs_buf.at[p], rs_send.at[k], rs_recv.at[p], where, MESH)

    def ar(k):
        p, where = along(k)
        return pltpu.make_async_remote_copy(
            part.at[0], z_buf.at[z], z_send.at[k], z_recv.at[z], where, MESH)

    def ar_in(k):
        p, where = along(k)
        return pltpu.make_async_remote_copy(
            part.at[0], z_buf.at[p], z_send.at[k], z_recv.at[p], where, MESH)

    def ag(k):
        p, where = plane(k)
        return pltpu.make_async_remote_copy(
            part.at[1], put_ref.at[own], ag_send.at[k], ag_recv.at[own], where, MESH)

    def ag_in(k):
        p, where = plane(k)
        return pltpu.make_async_remote_copy(
            part.at[1], put_ref.at[p], ag_send.at[k], ag_recv.at[p], where, MESH)

    def each(lo, hi, what):
        def body(k, _):
            what(k)
            return 0
        lax.fori_loop(lo, hi, body, 0)

    each(1, 32, lambda k: rs(k)[1].start())
    rs_buf[own] = fg_ref[own]
    each(1, 32, lambda k: rs_in(k).wait_recv())
    total = rs_buf[0]
    for p in range(1, 32):
        total = total + rs_buf[p]
    part[0] = total
    each(1, 8, lambda k: ar(k).start())
    z_buf[z] = total
    each(1, 8, lambda k: ar_in(k).wait_recv())
    total = z_buf[0]
    for p in range(1, 8):
        total = total + z_buf[p]
    part[1] = total
    each(1, 32, lambda k: ag(k).start())
    put_ref[own] = total
    each(1, 32, lambda k: ag_in(k).wait_recv())
    each(1, 32, lambda k: rs(k)[1].wait_send())
    each(1, 8, lambda k: ar(k).wait_send())
    each(1, 32, lambda k: ag(k).wait_send())


def greet_reducers():
    barrier = pltpu.get_barrier_semaphore()
    ctx = lax.axis_index("ctx")
    own = lax.axis_index("dp") * 8 + lax.rem(ctx, 8)
    z = ctx // 8

    def plane(k, _):
        p = lax.rem(own + k, 32)
        pl.semaphore_signal(barrier, 1, device_id={"dp": p // 8, "ctx": z * 8 + lax.rem(p, 8)}, device_id_type=MESH)
        return 0

    def along(k, _):
        p = lax.rem(z + k, 8)
        pl.semaphore_signal(barrier, 1, device_id={"ctx": p * 8 + lax.rem(ctx, 8)}, device_id_type=MESH)
        return 0

    lax.fori_loop(1, 32, plane, 0)
    lax.fori_loop(1, 8, along, 0)
    return barrier


AR_SCRATCH = [
    pltpu.VMEM((32, 4, 128), F32),
    pltpu.VMEM((8, 4, 128), F32),
    pltpu.VMEM((2, 4, 128), F32),
] + [pltpu.SemaphoreType.DMA((n,)) for n in (32, 32, 8, 8, 32, 32)]


def sum_kernel(fg_ref, put_ref, rs_buf, z_buf, part, *sems):
    barrier = greet_reducers()
    pl.semaphore_wait(barrier, 38)
    reduce_everywhere(fg_ref, put_ref, rs_buf, z_buf, part, sems)


def sum_everywhere(fg):
    vmem = pl.BlockSpec(memory_space=pltpu.VMEM)
    return pl.pallas_call(
        sum_kernel,
        out_shape=jax.ShapeDtypeStruct((32, 4, 128), F32),
        in_specs=[vmem],
        out_specs=vmem,
        scratch_shapes=AR_SCRATCH,
        compiler_params=pltpu.CompilerParams(collective_id=0, has_side_effects=True),
        name="sum_everywhere",
    )(fg)


def keeps(starts, ctx):
    own = jnp.any(starts == ctx * 128)
    after = jnp.any(starts == (ctx + 1) * 128) | (ctx == 63)
    return jnp.where(own, 0.0, 1.0).astype(BF16), jnp.where(after, 0.0, 1.0).astype(BF16)


def per_device(gate_in, key_in, value_in, cotangent, doc_starts, filters):
    q, k, v, c = gate_in[0], key_in[0], value_in[0], cotangent[0]
    keep_own, keep_after = keeps(doc_starts[0], lax.axis_index("ctx"))
    u = (k.astype(F32) * v.astype(F32)).astype(BF16) * keep_after
    dy = (c.astype(F32) * q.astype(F32)).astype(BF16) * keep_own
    up = lax.ppermute(u, "ctx", [(i, (i + 1) % 64) for i in range(64)])
    dn = lax.ppermute(dy, "ctx", [(i, (i - 1) % 64) for i in range(64)])
    z, gq, gk, gv, fg = tile_ops(filters, q, k, v, c, up, dn)
    total = sum_everywhere(fg).reshape(128, 128)
    return z[None], gq[None], gk[None], gv[None], total


def solution(mesh):
    rows = P("dp", "ctx", None)
    return jax.shard_map(
        per_device,
        mesh=mesh,
        in_specs=(rows, rows, rows, rows, P("dp", None), P()),
        out_specs=(rows, rows, rows, rows, P()),
        check_vma=False,
    )
```

```python
import itertools

import jax
import jax.numpy as jnp
from jax import lax
from jax.experimental import pallas as pl
from jax.experimental.pallas import tpu as pltpu
from jax.sharding import PartitionSpec as P

F32, BF16 = jnp.float32, jnp.bfloat16
MESH = pl.DeviceIdType.MESH
NT = (((1,), (1,)), ((), ()))


def build_bases(h_ref, hs_ref, b1_ref, b2_ref):
    lane = lax.broadcasted_iota(jnp.int32, (128, 128), 1)
    sub = lax.broadcasted_iota(jnp.int32, (128, 128), 0)
    flip = (lane + sub == 127).astype(BF16)
    h = h_ref[...]
    hs_ref[0] = h.astype(F32)
    hs_ref[1] = jnp.dot(h, flip, preferred_element_type=F32)
    r = lax.broadcasted_iota(jnp.int32, (16, 128), 0)
    m = lax.broadcasted_iota(jnp.int32, (16, 128), 1)

    def step(i, _):
        for j in range(8):
            f = i * 8 + j
            rows = pl.ds(pl.multiple_of(f * 16, 16), 16)
            fwd = jnp.broadcast_to(hs_ref[0, pl.ds(f, 1), :], (16, 128))
            rev = jnp.broadcast_to(hs_ref[1, pl.ds(f, 1), :], (16, 128))
            fwd = pltpu.roll(fwd, 0, 1, stride=1, stride_axis=0)
            rev = pltpu.roll(rev, 1, 1, stride=1, stride_axis=0)
            b2_ref[rows, 0:128] = jnp.where(m >= r, fwd, 0.0).astype(BF16)
            b2_ref[rows, 128:256] = jnp.where(m < r, fwd, 0.0).astype(BF16)
            b1_ref[rows, 0:128] = jnp.where(m >= r + 1, rev, 0.0).astype(BF16)
            b1_ref[rows, 128:256] = jnp.where(m < r + 1, rev, 0.0).astype(BF16)
        return 0

    lax.fori_loop(0, 16, step, 0)


def pick(full, half, group):
    lanes = slice(128 * half, 128 * half + 128)
    out = full[112:128, lanes]
    for g in range(6, -1, -1):
        out = jnp.where(group == g, full[16 * g : 16 * g + 16, lanes], out)
    return out


def slab(ref, a, blk):
    return jnp.concatenate(
        [ref[16 * a : 16 * a + 144, blk], ref[16 * a + 16 : 16 * a + 160, blk]], axis=1
    )


def block_of(i):
    return pl.ds(pl.multiple_of(i * 128, 128), 128)


def lane_group():
    return lax.broadcasted_iota(jnp.int32, (16, 128), 1) // 16


def conv_block(i, q_ref, k_ref, v_ref, c_ref, u_ref, d_ref, b1_ref, b2_ref, outs):
    z_ref, gq_ref, gk_ref, gv_ref = outs
    blk = block_of(i)
    group = lane_group()
    lhs1 = b1_ref[blk, 0:144]
    lhs2 = b2_ref[blk, 0:144]
    for a in range(0, 8, 2):
        y = jnp.dot(lhs1, slab(u_ref, a, blk), preferred_element_type=F32)
        du = jnp.dot(lhs2, slab(d_ref, a, blk), preferred_element_type=F32)
        for half in range(2):
            rows = slice(16 * (a + half), 16 * (a + half) + 16)
            yv = pick(y, half, group)
            z_ref[rows, blk] = (q_ref[rows, blk].astype(F32) * yv).astype(BF16)
            gq_ref[rows, blk] = (c_ref[rows, blk].astype(F32) * yv).astype(BF16)
            dv = pick(du, half, group)
            gk_ref[rows, blk] = (v_ref[rows, blk].astype(F32) * dv).astype(BF16)
            gv_ref[rows, blk] = (k_ref[rows, blk].astype(F32) * dv).astype(BF16)


def pair_sums(i, u_ref, d_ref, g_ref):
    blk = block_of(i)
    group = lane_group()
    total = jnp.zeros((128, 144), F32)
    for a in range(0, 8, 2):
        pair = []
        for half in range(2):
            start = 128 + 16 * (a + half)
            rows = u_ref[start : start + 16, blk]
            spread = [jnp.where(group == g, rows, jnp.zeros_like(rows)) for g in range(8)]
            pair.append(jnp.concatenate(spread, axis=0))
        total = total + lax.dot_general(
            jnp.concatenate(pair, axis=1), slab(d_ref, a, blk), NT, preferred_element_type=F32
        )
    g_ref[blk, 0:144] = total


def diagonals(i, g_ref):
    rows = block_of(i)
    lane = lax.broadcasted_iota(jnp.int32, (128, 128), 1)
    r = lax.broadcasted_iota(jnp.int32, (128, 128), 0) % 16
    both = jnp.where(lane < r, g_ref[rows, 128:256], g_ref[rows, 0:128])
    parts = [
        both[16 * f : 16 * f + 8] + pltpu.roll(both[16 * f + 8 : 16 * f + 16], 120, 1)
        for f in range(8)
    ]
    sub = lax.broadcasted_iota(jnp.int32, (8, 128), 0)
    for step in (4, 2, 1):
        low = sub % (2 * step) < step
        merged = []
        for f in range(step):
            one, two = parts[f], parts[f + step]
            first = jnp.where(low, one, pltpu.roll(two, step, 0))
            second = jnp.where(low, pltpu.roll(one, 8 - step, 0), two)
            merged.append(first + pltpu.roll(second, 128 - step, 1))
        parts = merged
    return parts[0]


CHUNKS = 8
WIDE = 2048 // CHUNKS
SIZES = {"y": 4, "z": 8, "x": 4, "core": 2}
PLANE, LINE = ("y", "x", "core"), ("z",)


def place():
    ctx = lax.axis_index("ctx")
    return {
        "y": lax.axis_index("dp"),
        "z": ctx // 8,
        "x": lax.rem(ctx // 2, 4),
        "core": lax.rem(ctx, 2),
    }


def device(at):
    return {"dp": at["y"], "ctx": (at["z"] * 4 + at["x"]) * 2 + at["core"]}


def index_in(axes, at):
    index = 0
    for axis in axes:
        index = index * SIZES[axis] + at[axis]
    return index


def others(axes):
    def hops(offset):
        return sum(
            0.1 * d if axis == "core" else min(d, SIZES[axis] - d)
            for axis, d in zip(axes, offset)
        )

    every = itertools.product(*[range(SIZES[axis]) for axis in axes])
    return sorted([o for o in every if any(o)], key=lambda o: -hops(o))


def shifted(axes, at, offset):
    at = dict(at)
    for axis, d in zip(axes, offset):
        if d:
            at[axis] = lax.rem(at[axis] + d, SIZES[axis])
    return at


def beside(by):
    return {"ctx": lax.rem(lax.axis_index("ctx") + 64 + by, 64)}


def greet(at):
    barrier = pltpu.get_barrier_semaphore()
    count = 0
    for by in (1, -1):
        pl.semaphore_signal(barrier, 1, device_id=beside(by), device_id_type=MESH)
        count += 1
    for axes in (PLANE, LINE):
        for offset in others(axes):
            pl.semaphore_signal(
                barrier, 1, device_id=device(shifted(axes, at, offset)), device_id_type=MESH)
            count += 1
    return barrier, count


def send_all(axes, at, src_of, dst, send, recv):
    own = index_in(axes, at)
    for offset in others(axes):
        there = shifted(axes, at, offset)
        pltpu.make_async_remote_copy(
            src_of(index_in(axes, there)), dst.at[own], send, recv, device(there), MESH).start()


def wait_all(dst, sem):
    most = dst.at[pl.ds(0, dst.shape[0] - 1)]
    pltpu.make_async_copy(most, most, sem).wait()


def tree_sum(ref):
    terms = [ref[i] for i in range(ref.shape[0])]
    while len(terms) > 1:
        terms = [sum(terms[i : i + 2]) for i in range(0, len(terms), 2)]
    return terms[0]


def keep_of(starts_ref, position):
    hit = starts_ref[0, 0] == position
    for i in range(1, 17):
        hit = jnp.logical_or(hit, starts_ref[0, i] == position)
    return jnp.where(hit, 0.0, 1.0)


def whole_kernel(h_hbm, s_hbm, q_hbm, k_hbm, v_hbm, c_hbm,
                 z_ref, gq_ref, gk_ref, gv_ref, put_ref,
                 h_ref, s_ref, q_ref, k_ref, v_ref, c_ref,
                 u_ref, d_ref, us_ref, ds_ref, b1_ref, b2_ref, hs_ref, g_ref,
                 fg_ref, rs_buf, z_buf, part, loads,
                 u_send, u_recv, d_send, d_recv, sums):
    at = place()
    ctx = lax.axis_index("ctx")
    barrier, greeted = greet(at)
    pairs = ((h_hbm, h_ref), (s_hbm, s_ref), (k_hbm, k_ref), (v_hbm, v_ref), (q_hbm, q_ref), (c_hbm, c_ref))
    copies = [pltpu.make_async_copy(src, dst, loads.at[i]) for i, (src, dst) in enumerate(pairs)]
    for copy in copies:
        copy.start()
    for copy in copies[1:]:
        copy.wait()
    keep_own = keep_of(s_ref, ctx * 128)
    keep_after = keep_of(s_ref, (ctx + 1) * 128) * jnp.where(ctx == 63, 0.0, 1.0)

    def products(i, _):
        rows = pl.ds(pl.multiple_of(i * 16, 16), 16)
        below = pl.ds(pl.multiple_of(i * 16 + 128, 16), 16)
        u = k_ref[rows, :].astype(F32) * v_ref[rows, :].astype(F32)
        u_ref[below, :] = u.astype(BF16)
        us_ref[rows, :] = (u * keep_after).astype(BF16)
        dy = c_ref[rows, :].astype(F32) * q_ref[rows, :].astype(F32)
        d_ref[rows, :] = dy.astype(BF16)
        ds_ref[rows, :] = (dy * keep_own).astype(BF16)
        return 0

    lax.fori_loop(0, 8, products, 0)
    pl.semaphore_wait(barrier, greeted)

    def halo(j, by):
        lanes = pl.ds(pl.multiple_of(j * WIDE, WIDE), WIDE)
        if by == 1:
            return pltpu.make_async_remote_copy(
                us_ref.at[:, lanes], u_ref.at[pl.ds(0, 128), lanes],
                u_send.at[j], u_recv.at[j], beside(1), MESH)
        return pltpu.make_async_remote_copy(
            ds_ref.at[:, lanes], d_ref.at[pl.ds(128, 128), lanes],
            d_send.at[j], d_recv.at[j], beside(-1), MESH)

    def start(j, _):
        halo(j, -1).start()
        halo(j, 1).start()
        return 0

    lax.fori_loop(0, CHUNKS, start, 0)
    copies[0].wait()
    build_bases(h_ref, hs_ref, b1_ref, b2_ref)
    per = 16 // CHUNKS

    def sums_of(j):
        for i in range(per):
            pair_sums(j * per + i, u_ref, d_ref, g_ref)

    def diagonals_of(j):
        for i in range(per):
            rows = diagonals(j * per + i, g_ref)
            slot = 2 * (j * per + i)
            fg_ref[slot] = rows[0:4]
            fg_ref[slot + 1] = rows[4:8]

    halo(0, -1).wait_recv()
    sums_of(0)

    def arrive(j, _):
        halo(j, -1).wait_recv()
        diagonals_of(j - 1)
        sums_of(j)
        return 0

    lax.fori_loop(1, CHUNKS, arrive, 0)
    diagonals_of(CHUNKS - 1)

    own, height = index_in(PLANE, at), index_in(LINE, at)
    send_all(PLANE, at, lambda p: fg_ref.at[p], rs_buf, sums.at[0], sums.at[1])
    rs_buf[own] = fg_ref[own]

    def late(j, _):
        halo(j, 1).wait_recv()
        return 0

    lax.fori_loop(0, CHUNKS, late, 0)
    outs = (z_ref, gq_ref, gk_ref, gv_ref)

    def convolve(i, _):
        conv_block(i, q_ref, k_ref, v_ref, c_ref, u_ref, d_ref, b1_ref, b2_ref, outs)
        return 0

    lax.fori_loop(0, 12, convolve, 0)
    wait_all(rs_buf, sums.at[1])
    part[0] = tree_sum(rs_buf)
    send_all(LINE, at, lambda p: part.at[0], z_buf, sums.at[2], sums.at[3])
    z_buf[height] = part[0]
    lax.fori_loop(12, 16, convolve, 0)
    wait_all(z_buf, sums.at[3])
    part[1] = tree_sum(z_buf)
    send_all(PLANE, at, lambda p: part.at[1], put_ref, sums.at[4], sums.at[5])
    put_ref[own] = part[1]

    def sent(j, _):
        halo(j, -1).wait_send()
        halo(j, 1).wait_send()
        return 0

    lax.fori_loop(0, CHUNKS, sent, 0)
    wait_all(rs_buf, sums.at[0])
    wait_all(z_buf, sums.at[2])
    wait_all(put_ref, sums.at[4])
    wait_all(put_ref, sums.at[5])


def whole(h, starts, q, k, v, c):
    sd = jax.ShapeDtypeStruct
    vmem = pl.BlockSpec(memory_space=pltpu.VMEM)
    hbm = pl.BlockSpec(memory_space=pl.ANY)
    act = pltpu.VMEM((128, 2048), BF16)
    two = pltpu.VMEM((256, 2048), BF16)
    base = pltpu.VMEM((2048, 256), BF16)
    dma = pltpu.SemaphoreType.DMA
    return pl.pallas_call(
        whole_kernel,
        out_shape=[pltpu.VMEM((128, 2048), BF16)] * 4 + [pltpu.VMEM((32, 4, 128), F32)],
        in_specs=[hbm] * 6,
        out_specs=[vmem] * 5,
        scratch_shapes=[
            pltpu.VMEM((128, 128), BF16), pltpu.SMEM((1, 17), jnp.int32), act, act, act, act,
            two, two, act, act, base, base,
            pltpu.VMEM((2, 128, 128), F32), pltpu.VMEM((2048, 256), F32),
            pltpu.VMEM((32, 4, 128), F32), pltpu.VMEM((32, 4, 128), F32),
            pltpu.VMEM((8, 4, 128), F32), pltpu.VMEM((2, 4, 128), F32),
            dma((6,)), dma((CHUNKS,)), dma((CHUNKS,)), dma((CHUNKS,)), dma((CHUNKS,)), dma((6,)),
        ],
        compiler_params=pltpu.CompilerParams(
            collective_id=0, has_side_effects=True, vmem_limit_bytes=VMEM_LIMIT),
        name="whole_operator",
    )(*[pltpu.with_memory_space_constraint(x, pltpu.HBM) for x in (h, starts, q, k, v, c)])


VMEM_LIMIT = 32 * 1024 * 1024


def finish_kernel(*refs):
    sems = refs[10]
    copies = [pltpu.make_async_copy(refs[i], refs[5 + i], sems.at[i]) for i in range(5)]
    for copy in copies:
        copy.start()
    for copy in copies:
        copy.wait()


def finish(arrays):
    hbm = pl.BlockSpec(memory_space=pl.ANY)
    return pl.pallas_call(
        finish_kernel,
        out_shape=[pltpu.HBM(a.shape, a.dtype) for a in arrays],
        in_specs=[hbm] * 5,
        out_specs=[hbm] * 5,
        scratch_shapes=[pltpu.SemaphoreType.DMA((5,))],
        compiler_params=pltpu.CompilerParams(vmem_limit_bytes=1024 * 1024),
        name="finish",
    )(*[pltpu.with_memory_space_constraint(a, pltpu.VMEM) for a in arrays])


def per_device(gate_in, key_in, value_in, cotangent, doc_starts, filters):
    z, gq, gk, gv, put = finish(whole(
        filters, doc_starts, gate_in[0], key_in[0], value_in[0], cotangent[0]))
    return z[None], gq[None], gk[None], gv[None], put.reshape(128, 128)


def solution(mesh):
    rows = P("dp", "ctx", None)
    return jax.shard_map(
        per_device,
        mesh=mesh,
        in_specs=(rows, rows, rows, rows, P("dp", None), P()),
        out_specs=(rows, rows, rows, rows, P()),
        check_vma=False,
    )
```

```python
import itertools

import jax
import jax.numpy as jnp
from jax import lax
from jax.experimental import pallas as pl
from jax.experimental.pallas import tpu as pltpu
from jax.sharding import PartitionSpec as P

F32, BF16 = jnp.float32, jnp.bfloat16
MESH = pl.DeviceIdType.MESH
NT = (((1,), (1,)), ((), ()))


def build_bases(h_ref, hs_ref, b1_ref, b2_ref):
    lane = lax.broadcasted_iota(jnp.int32, (128, 128), 1)
    sub = lax.broadcasted_iota(jnp.int32, (128, 128), 0)
    flip = (lane + sub == 127).astype(BF16)
    h = h_ref[...]
    hs_ref[0] = h.astype(F32)
    hs_ref[1] = jnp.dot(h, flip, preferred_element_type=F32)
    r = lax.broadcasted_iota(jnp.int32, (16, 128), 0)
    m = lax.broadcasted_iota(jnp.int32, (16, 128), 1)

    def step(i, _):
        for j in range(8):
            f = i * 8 + j
            rows = pl.ds(pl.multiple_of(f * 16, 16), 16)
            fwd = jnp.broadcast_to(hs_ref[0, pl.ds(f, 1), :], (16, 128))
            rev = jnp.broadcast_to(hs_ref[1, pl.ds(f, 1), :], (16, 128))
            fwd = pltpu.roll(fwd, 0, 1, stride=1, stride_axis=0)
            rev = pltpu.roll(rev, 1, 1, stride=1, stride_axis=0)
            b2_ref[rows, 0:128] = jnp.where(m >= r, fwd, 0.0).astype(BF16)
            b2_ref[rows, 128:256] = jnp.where(m < r, fwd, 0.0).astype(BF16)
            b1_ref[rows, 0:128] = jnp.where(m >= r + 1, rev, 0.0).astype(BF16)
            b1_ref[rows, 128:256] = jnp.where(m < r + 1, rev, 0.0).astype(BF16)
        return 0

    lax.fori_loop(0, 16, step, 0)


def pick(full, half, group):
    lanes = slice(128 * half, 128 * half + 128)
    out = full[112:128, lanes]
    for g in range(6, -1, -1):
        out = jnp.where(group == g, full[16 * g : 16 * g + 16, lanes], out)
    return out


def slab(ref, a, blk):
    return jnp.concatenate(
        [ref[16 * a : 16 * a + 144, blk], ref[16 * a + 16 : 16 * a + 160, blk]], axis=1
    )


def block_of(i):
    return pl.ds(pl.multiple_of(i * 128, 128), 128)


def lane_group():
    return lax.broadcasted_iota(jnp.int32, (16, 128), 1) // 16


def conv_block(i, bases, source, gates, results):
    blk = block_of(i)
    group = lane_group()
    lhs = bases[blk, 0:144]
    for a in range(0, 8, 2):
        full = jnp.dot(lhs, slab(source, a, blk), preferred_element_type=F32)
        for half in range(2):
            rows = slice(16 * (a + half), 16 * (a + half) + 16)
            value = pick(full, half, group)
            for gate, result in zip(gates, results):
                result[rows, blk] = (gate[rows, blk].astype(F32) * value).astype(BF16)


def pair_sums(i, slot, rows_ref, first, slab_ref, g_ref):
    blk = block_of(i)
    group = lane_group()
    total = jnp.zeros((128, 144), F32)
    for a in range(0, 8, 2):
        pair = []
        for half in range(2):
            start = first + 16 * (a + half)
            rows = rows_ref[start : start + 16, blk]
            spread = [jnp.where(group == g, rows, jnp.zeros_like(rows)) for g in range(8)]
            pair.append(jnp.concatenate(spread, axis=0))
        total = total + lax.dot_general(
            jnp.concatenate(pair, axis=1), slab(slab_ref, a, blk), NT, preferred_element_type=F32
        )
    g_ref[slot, :, 0:144] = total


def diagonals(slot, g_ref, shift):
    lane = lax.broadcasted_iota(jnp.int32, (128, 128), 1)
    r = lax.broadcasted_iota(jnp.int32, (128, 128), 0) % 16
    both = jnp.where(lane < r + shift, g_ref[slot, :, 128:256], g_ref[slot, :, 0:128])
    parts = [
        both[16 * f : 16 * f + 8] + pltpu.roll(both[16 * f + 8 : 16 * f + 16], 120, 1)
        for f in range(8)
    ]
    sub = lax.broadcasted_iota(jnp.int32, (8, 128), 0)
    for step in (4, 2, 1):
        low = sub % (2 * step) < step
        merged = []
        for f in range(step):
            one, two = parts[f], parts[f + step]
            first = jnp.where(low, one, pltpu.roll(two, step, 0))
            second = jnp.where(low, pltpu.roll(one, 8 - step, 0), two)
            merged.append(first + pltpu.roll(second, 128 - step, 1))
        parts = merged
    return parts[0]


CHUNKS = 8
HALF = CHUNKS // 2
WIDE = 2048 // CHUNKS
SIZES = {"y": 4, "z": 8, "x": 4, "core": 2}
PLANE, LINE = ("y", "x"), ("z", "core")


def place():
    ctx = lax.axis_index("ctx")
    return {
        "y": lax.axis_index("dp"),
        "z": ctx // 8,
        "x": lax.rem(ctx // 2, 4),
        "core": lax.rem(ctx, 2),
    }


def device(at):
    return {"dp": at["y"], "ctx": (at["z"] * 4 + at["x"]) * 2 + at["core"]}


def index_in(axes, at):
    index = 0
    for axis in axes:
        index = index * SIZES[axis] + at[axis]
    return index


def others(axes):
    def hops(offset):
        return sum(
            0.1 * d if axis == "core" else min(d, SIZES[axis] - d)
            for axis, d in zip(axes, offset)
        )

    every = itertools.product(*[range(SIZES[axis]) for axis in axes])
    return sorted([o for o in every if any(o)], key=lambda o: -hops(o))


def shifted(axes, at, offset):
    at = dict(at)
    for axis, d in zip(axes, offset):
        if d:
            at[axis] = lax.rem(at[axis] + d, SIZES[axis])
    return at


def beside(by):
    return {"ctx": lax.rem(lax.axis_index("ctx") + 64 + by, 64)}


def greet(at):
    barrier = pltpu.get_barrier_semaphore()
    count = 0
    for by in (1, -1):
        pl.semaphore_signal(barrier, 1, device_id=beside(by), device_id_type=MESH)
        count += 1
    for axes in (PLANE, LINE):
        for offset in others(axes):
            pl.semaphore_signal(
                barrier, 1, device_id=device(shifted(axes, at, offset)), device_id_type=MESH)
            count += 1
    return barrier, count


def group_of(at, step):
    return lax.rem(at["y"] + (2, 1, 3, 0)[step], 4)


def chunk_of(at, step):
    return group_of(at, step % HALF) + (HALF if step >= HALF else 0)


def block_at(y, x):
    return 2 * y + x + jnp.where(x >= 2, 6, 0)


def send_all(axes, at, src_of, dst, send, recv):
    own = index_in(axes, at)
    for offset in others(axes):
        there = shifted(axes, at, offset)
        pltpu.make_async_remote_copy(
            src_of(index_in(axes, there)), dst.at[own], send, recv, device(there), MESH).start()


def wait_all(dst, sem):
    most = dst.at[pl.ds(0, dst.shape[0] - 1)]
    pltpu.make_async_copy(most, most, sem).wait()


def tree_sum(ref):
    terms = [ref[i] for i in range(ref.shape[0])]
    while len(terms) > 1:
        terms = [sum(terms[i : i + 2]) for i in range(0, len(terms), 2)]
    return terms[0]


def keep_of(starts_ref, position):
    hit = starts_ref[0, 0] == position
    for i in range(1, 17):
        hit = jnp.logical_or(hit, starts_ref[0, i] == position)
    return jnp.where(hit, 0.0, 1.0)


def whole_kernel(h_hbm, s_hbm, q_hbm, k_hbm, v_hbm, c_hbm,
                 z_ref, gq_ref, gk_ref, gv_ref, put_ref,
                 h_ref, s_ref, q_ref, k_ref, v_ref, c_ref,
                 u_ref, d_ref, us_ref, ds_ref, b1_ref, b2_ref, hs_ref, g_ref,
                 fg_ref, rs_buf, z_buf, part, loads,
                 u_send, u_recv, d_send, d_recv, sums):
    at = place()
    ctx = lax.axis_index("ctx")
    barrier, greeted = greet(at)
    small = [
        pltpu.make_async_copy(s_hbm, s_ref, loads.at[0]),
        pltpu.make_async_copy(h_hbm, h_ref, loads.at[1]),
    ]

    def lanes_of(j):
        return pl.ds(pl.multiple_of(j * WIDE, WIDE), WIDE)

    def load(n, j):
        src, dst = ((q_hbm, q_ref), (c_hbm, c_ref), (k_hbm, k_ref), (v_hbm, v_ref))[n]
        return pltpu.make_async_copy(
            src.at[:, lanes_of(j)], dst.at[:, lanes_of(j)], loads.at[2 + n * CHUNKS + j])

    small[0].start()
    for step in range(CHUNKS):
        dy_chunk = chunk_of(at, step)
        u_chunk = chunk_of(at, (step + HALF) % CHUNKS)
        for n, j in ((0, dy_chunk), (1, dy_chunk), (2, u_chunk), (3, u_chunk)):
            load(n, j).start()
        if step == 0:
            small[1].start()
    small[0].wait()
    keep_own = keep_of(s_ref, ctx * 128)
    keep_after = keep_of(s_ref, (ctx + 1) * 128) * jnp.where(ctx == 63, 0.0, 1.0)

    def dy_product(j):
        load(0, j).wait()
        load(1, j).wait()
        lanes = lanes_of(j)
        dy = c_ref[:, lanes].astype(F32) * q_ref[:, lanes].astype(F32)
        d_ref[0:128, lanes] = dy.astype(BF16)
        ds_ref[:, lanes] = (dy * keep_own).astype(BF16)

    def u_product(j):
        load(2, j).wait()
        load(3, j).wait()
        lanes = lanes_of(j)
        u = k_ref[:, lanes].astype(F32) * v_ref[:, lanes].astype(F32)
        u_ref[128:256, lanes] = u.astype(BF16)
        us_ref[:, lanes] = (u * keep_after).astype(BF16)

    def halo(j, by):
        lanes = lanes_of(j)
        if by == 1:
            return pltpu.make_async_remote_copy(
                us_ref.at[:, lanes], u_ref.at[pl.ds(0, 128), lanes],
                u_send.at[j], u_recv.at[j], beside(1), MESH)
        return pltpu.make_async_remote_copy(
            ds_ref.at[:, lanes], d_ref.at[pl.ds(128, 128), lanes],
            d_send.at[j], d_recv.at[j], beside(-1), MESH)

    for step in range(HALF):
        dy_chunk, u_chunk = chunk_of(at, step), chunk_of(at, step + HALF)
        dy_product(dy_chunk)
        u_product(u_chunk)
        if step == 0:
            pl.semaphore_wait(barrier, greeted)
        halo(dy_chunk, -1).start()
        halo(u_chunk, 1).start()
    for step in range(HALF):
        dy_product(chunk_of(at, step + HALF))
        u_product(chunk_of(at, step))
    small[1].wait()
    build_bases(h_ref, hs_ref, b1_ref, b2_ref)
    lane = lax.broadcasted_iota(jnp.int32, (128, 128), 1)
    sub = lax.broadcasted_iota(jnp.int32, (128, 128), 0)
    turn = jnp.where(lane + sub == 128, 1.0, jnp.where(lane + sub == 0, 1.0, 0.0))
    per = 8 // HALF

    def sums_of(step, j):
        for i in range(per):
            slot = 2 * (per * step + i)
            pair_sums(j * per + i, slot, u_ref, 128, d_ref, g_ref)
            pair_sums(8 + j * per + i, slot + 1, d_ref, 0, u_ref, g_ref)

    def diagonals_of(step, j):
        back = []
        for i in range(per):
            slot = 2 * (per * step + i)
            fg_ref[j * per + i] = diagonals(slot, g_ref, 0)
            back.append(diagonals(slot + 1, g_ref, 1))
        back = jnp.dot(
            jnp.concatenate(back, axis=0), turn,
            precision=lax.Precision.HIGHEST, preferred_element_type=F32)
        for i in range(per):
            fg_ref[8 + j * per + i] = back[8 * i : 8 * i + 8]

    own = at["y"] * 4 + at["x"]
    mine = block_at(at["y"], at["x"])
    height = index_in(LINE, at)

    def hand_over(j, last):
        for dx in (2, 1, 3) if last else (2, 1, 3, 0):
            x = lax.rem(at["x"] + dx, 4)
            there = device({"y": j, "z": at["z"], "x": x, "core": at["core"]})
            pltpu.make_async_remote_copy(
                fg_ref.at[block_at(j, x)], rs_buf.at[own], sums.at[0], sums.at[1], there, MESH
            ).start()

    before = None
    for step in range(HALF):
        j = group_of(at, step)
        halo(j, -1).wait_recv()
        halo(j + HALF, 1).wait_recv()
        if before is not None:
            diagonals_of(step - 1, before)
        sums_of(step, j)
        if before is not None:
            hand_over(before, False)
        before = j
    diagonals_of(HALF - 1, before)
    hand_over(before, True)
    rs_buf[own] = fg_ref[mine]
    for step in range(HALF):
        halo(chunk_of(at, step + HALF), -1).start()
        halo(chunk_of(at, step), 1).start()

    def outputs(i):
        conv_block(i, b1_ref, u_ref, (q_ref, c_ref), (z_ref, gq_ref))

    def gradients(i):
        conv_block(i, b2_ref, d_ref, (v_ref, k_ref), (gk_ref, gv_ref))

    def early(i, _):
        outputs(8 + i)
        gradients(i)
        return 0

    def later(i, _):
        outputs(i)
        gradients(8 + i)
        return 0

    lax.fori_loop(0, SPLIT[0], early, 0)
    wait_all(rs_buf, sums.at[1])
    part[0] = tree_sum(rs_buf)
    send_all(LINE, at, lambda p: part.at[0], z_buf, sums.at[2], sums.at[3])
    z_buf[height] = part[0]
    lax.fori_loop(SPLIT[0], 8, early, 0)

    def last_halo(j, _):
        halo(j + HALF, -1).wait_recv()
        halo(j, 1).wait_recv()
        return 0

    lax.fori_loop(0, HALF, last_halo, 0)
    lax.fori_loop(0, SPLIT[1], later, 0)
    wait_all(z_buf, sums.at[3])
    part[1] = tree_sum(z_buf)
    for offset in others(PLANE):
        there = device(shifted(PLANE, at, offset))
        pltpu.make_async_remote_copy(
            part.at[1], put_ref.at[mine], sums.at[4], sums.at[5], there, MESH).start()
    put_ref[mine] = part[1]
    lax.fori_loop(SPLIT[1], 8, later, 0)

    def sent(j, _):
        halo(j, -1).wait_send()
        halo(j, 1).wait_send()
        return 0

    lax.fori_loop(0, CHUNKS, sent, 0)
    wait_all(rs_buf, sums.at[0])
    wait_all(z_buf, sums.at[2])
    wait_all(put_ref, sums.at[4])
    wait_all(put_ref, sums.at[5])


SPLIT = (6, 6)


def whole(h, starts, q, k, v, c):
    sd = jax.ShapeDtypeStruct
    vmem = pl.BlockSpec(memory_space=pltpu.VMEM)
    hbm = pl.BlockSpec(memory_space=pl.ANY)
    act = pltpu.VMEM((128, 2048), BF16)
    two = pltpu.VMEM((256, 2048), BF16)
    base = pltpu.VMEM((2048, 256), BF16)
    dma = pltpu.SemaphoreType.DMA
    return pl.pallas_call(
        whole_kernel,
        out_shape=[pltpu.VMEM((128, 2048), BF16)] * 4 + [pltpu.VMEM((16, 8, 128), F32)],
        in_specs=[hbm] * 6,
        out_specs=[vmem] * 5,
        scratch_shapes=[
            pltpu.VMEM((128, 128), BF16), pltpu.SMEM((1, 17), jnp.int32), act, act, act, act,
            two, two, act, act, base, base,
            pltpu.VMEM((2, 128, 128), F32), pltpu.VMEM((16, 128, 256), F32),
            pltpu.VMEM((16, 8, 128), F32), pltpu.VMEM((16, 8, 128), F32),
            pltpu.VMEM((16, 8, 128), F32), pltpu.VMEM((2, 8, 128), F32),
            dma((2 + 4 * CHUNKS,)), dma((CHUNKS,)), dma((CHUNKS,)), dma((CHUNKS,)), dma((CHUNKS,)), dma((6,)),
        ],
        compiler_params=pltpu.CompilerParams(
            collective_id=0, has_side_effects=True, vmem_limit_bytes=VMEM_LIMIT),
        name="whole_operator",
    )(*[pltpu.with_memory_space_constraint(x, pltpu.HBM) for x in (h, starts, q, k, v, c)])


VMEM_LIMIT = 32 * 1024 * 1024


def finish_kernel(*refs):
    sems = refs[10]
    copies = [pltpu.make_async_copy(refs[i], refs[5 + i], sems.at[i]) for i in range(5)]
    for copy in copies:
        copy.start()
    for copy in copies:
        copy.wait()


def finish(arrays):
    hbm = pl.BlockSpec(memory_space=pl.ANY)
    return pl.pallas_call(
        finish_kernel,
        out_shape=[pltpu.HBM(a.shape, a.dtype) for a in arrays],
        in_specs=[hbm] * 5,
        out_specs=[hbm] * 5,
        scratch_shapes=[pltpu.SemaphoreType.DMA((5,))],
        compiler_params=pltpu.CompilerParams(vmem_limit_bytes=1024 * 1024),
        name="finish",
    )(*[pltpu.with_memory_space_constraint(a, pltpu.VMEM) for a in arrays])


def per_device(gate_in, key_in, value_in, cotangent, doc_starts, filters):
    z, gq, gk, gv, put = finish(whole(
        filters, doc_starts, gate_in[0], key_in[0], value_in[0], cotangent[0]))
    return z[None], gq[None], gk[None], gv[None], put.reshape(128, 128)


def solution(mesh):
    rows = P("dp", "ctx", None)
    return jax.shard_map(
        per_device,
        mesh=mesh,
        in_specs=(rows, rows, rows, rows, P("dp", None), P()),
        out_specs=(rows, rows, rows, rows, P()),
        check_vma=False,
    )
```

```python
import itertools

import jax
import jax.numpy as jnp
from jax import lax
from jax.experimental import pallas as pl
from jax.experimental.pallas import tpu as pltpu
from jax.sharding import PartitionSpec as P

F32, BF16 = jnp.float32, jnp.bfloat16
MESH = pl.DeviceIdType.MESH
NT = (((1,), (1,)), ((), ()))


def build_bases(h_ref, hs_ref, b1_ref, b2_ref):
    lane = lax.broadcasted_iota(jnp.int32, (128, 128), 1)
    sub = lax.broadcasted_iota(jnp.int32, (128, 128), 0)
    flip = (lane + sub == 127).astype(BF16)
    h = h_ref[...]
    hs_ref[0] = h.astype(F32)
    hs_ref[1] = jnp.dot(h, flip, preferred_element_type=F32)
    r = lax.broadcasted_iota(jnp.int32, (16, 128), 0)
    m = lax.broadcasted_iota(jnp.int32, (16, 128), 1)

    def step(i, _):
        for j in range(8):
            f = i * 8 + j
            rows = pl.ds(pl.multiple_of(f * 16, 16), 16)
            fwd = jnp.broadcast_to(hs_ref[0, pl.ds(f, 1), :], (16, 128))
            rev = jnp.broadcast_to(hs_ref[1, pl.ds(f, 1), :], (16, 128))
            fwd = pltpu.roll(fwd, 0, 1, stride=1, stride_axis=0)
            rev = pltpu.roll(rev, 1, 1, stride=1, stride_axis=0)
            b2_ref[rows, 0:128] = jnp.where(m >= r, fwd, 0.0).astype(BF16)
            b2_ref[rows, 128:256] = jnp.where(m < r, fwd, 0.0).astype(BF16)
            b1_ref[rows, 0:128] = jnp.where(m >= r + 1, rev, 0.0).astype(BF16)
            b1_ref[rows, 128:256] = jnp.where(m < r + 1, rev, 0.0).astype(BF16)
        return 0

    lax.fori_loop(0, 16, step, 0)


def pick(full, half, group):
    lanes = slice(128 * half, 128 * half + 128)
    out = full[112:128, lanes]
    for g in range(6, -1, -1):
        out = jnp.where(group == g, full[16 * g : 16 * g + 16, lanes], out)
    return out


def slab(ref, a, blk):
    return jnp.concatenate(
        [ref[16 * a : 16 * a + 144, blk], ref[16 * a + 16 : 16 * a + 160, blk]], axis=1
    )


def block_of(i):
    return pl.ds(pl.multiple_of(i * 128, 128), 128)


def lane_group():
    return lax.broadcasted_iota(jnp.int32, (16, 128), 1) // 16


def conv_block(i, bases, source, gates, results):
    blk = block_of(i)
    group = lane_group()
    lhs = bases[blk, 0:144]
    for a in range(0, 8, 2):
        full = jnp.dot(lhs, slab(source, a, blk), preferred_element_type=F32)
        for half in range(2):
            rows = slice(16 * (a + half), 16 * (a + half) + 16)
            value = pick(full, half, group)
            for gate, result in zip(gates, results):
                result[rows, blk] = (gate[rows, blk].astype(F32) * value).astype(BF16)


def pair_sums(i, slot, rows_ref, first, slab_ref, g_ref):
    blk = block_of(i)
    group = lane_group()
    total = jnp.zeros((128, 144), F32)
    for a in range(0, 8, 2):
        pair = []
        for half in range(2):
            start = first + 16 * (a + half)
            rows = rows_ref[start : start + 16, blk]
            spread = [jnp.where(group == g, rows, jnp.zeros_like(rows)) for g in range(8)]
            pair.append(jnp.concatenate(spread, axis=0))
        total = total + lax.dot_general(
            jnp.concatenate(pair, axis=1), slab(slab_ref, a, blk), NT, preferred_element_type=F32
        )
    g_ref[slot, :, 0:144] = total


def diagonals(slot, g_ref, shift):
    lane = lax.broadcasted_iota(jnp.int32, (128, 128), 1)
    r = lax.broadcasted_iota(jnp.int32, (128, 128), 0) % 16
    both = jnp.where(lane < r + shift, g_ref[slot, :, 128:256], g_ref[slot, :, 0:128])
    parts = [
        both[16 * f : 16 * f + 8] + pltpu.roll(both[16 * f + 8 : 16 * f + 16], 120, 1)
        for f in range(8)
    ]
    sub = lax.broadcasted_iota(jnp.int32, (8, 128), 0)
    for step in (4, 2, 1):
        low = sub % (2 * step) < step
        merged = []
        for f in range(step):
            one, two = parts[f], parts[f + step]
            first = jnp.where(low, one, pltpu.roll(two, step, 0))
            second = jnp.where(low, pltpu.roll(one, 8 - step, 0), two)
            merged.append(first + pltpu.roll(second, 128 - step, 1))
        parts = merged
    return parts[0]


STEPS = ((0, 0, 2), (1, 0, 2), (2, 0, 2), (3, 0, 1), (3, 1, 1))
SIZES = {"y": 4, "z": 8, "x": 4, "core": 2}
PLANE, LINE = ("y", "x"), ("z", "core")


def place():
    ctx = lax.axis_index("ctx")
    return {
        "y": lax.axis_index("dp"),
        "z": ctx // 8,
        "x": lax.rem(ctx // 2, 4),
        "core": lax.rem(ctx, 2),
    }


def device(at):
    return {"dp": at["y"], "ctx": (at["z"] * 4 + at["x"]) * 2 + at["core"]}


def index_in(axes, at):
    index = 0
    for axis in axes:
        index = index * SIZES[axis] + at[axis]
    return index


def others(axes):
    def hops(offset):
        return sum(
            0.1 * d if axis == "core" else min(d, SIZES[axis] - d)
            for axis, d in zip(axes, offset)
        )

    every = itertools.product(*[range(SIZES[axis]) for axis in axes])
    return sorted([o for o in every if any(o)], key=lambda o: -hops(o))


def shifted(axes, at, offset):
    at = dict(at)
    for axis, d in zip(axes, offset):
        if d:
            at[axis] = lax.rem(at[axis] + d, SIZES[axis])
    return at


def beside(by):
    return {"ctx": lax.rem(lax.axis_index("ctx") + 64 + by, 64)}


NEAR = (("x", 1), ("x", 3), ("y", 1), ("y", 3), ("z", 1), ("z", 7), ("core", 1))


def only(by, act):
    ctx = lax.axis_index("ctx")
    pl.when(ctx < 63 if by == 1 else ctx > 0)(act)


def greet(at):
    barrier = pltpu.get_barrier_semaphore()
    for by in (1, -1):
        only(by, lambda: pl.semaphore_signal(
            barrier, 1, device_id=beside(by), device_id_type=MESH))
    for axis, by in NEAR:
        there = device(shifted((axis,), at, (by,)))
        pl.semaphore_signal(barrier, 1, device_id=there, device_id_type=MESH)
    ctx = lax.axis_index("ctx")
    at_end = jnp.logical_or(ctx == 0, ctx == 63)
    return barrier, jnp.where(at_end, 1, 2) + len(NEAR)


ROUNDS = (
    (("x", 3),),
    (("y", 1), ("y", 3)),
    (("y", 3),),
    (("z", 1), ("z", 7)),
    (("z", 1), ("z", 7)),
    (("z", 1), ("z", 7)),
    (("z", 7),),
)


def pass_on(at, known, n):
    for axis, by in ROUNDS[n]:
        there = device(shifted((axis,), at, (by,)))
        pl.semaphore_signal(known.at[n], 1, device_id=there, device_id_type=MESH)


def learn(known, n):
    pl.semaphore_wait(known.at[n], len(ROUNDS[n]))


def group_of(at, step):
    return lax.rem(at["y"] + (2, 1, 3, 0)[step], 4)


def block_at(y, x):
    return 2 * y + x + jnp.where(x >= 2, 6, 0)


def send_all(axes, at, src_of, dst, send, recv):
    own = index_in(axes, at)
    for offset in others(axes):
        there = shifted(axes, at, offset)
        pltpu.make_async_remote_copy(
            src_of(index_in(axes, there)), dst.at[own], send, recv, device(there), MESH).start()


def wait_all(dst, sem):
    most = dst.at[pl.ds(0, dst.shape[0] - 1)]
    pltpu.make_async_copy(most, most, sem).wait()


def tree_sum(ref):
    terms = [ref[i] for i in range(ref.shape[0])]
    while len(terms) > 1:
        terms = [sum(terms[i : i + 2]) for i in range(0, len(terms), 2)]
    return terms[0]


def keep_of(starts_ref, position):
    hit = starts_ref[0, 0] == position
    for i in range(1, 17):
        hit = jnp.logical_or(hit, starts_ref[0, i] == position)
    return jnp.where(hit, 0.0, 1.0)


def whole_kernel(h_hbm, s_hbm, q_hbm, k_hbm, v_hbm, c_hbm,
                 z_ref, gq_ref, gk_ref, gv_ref, put_ref,
                 h_ref, s_ref, q_ref, k_ref, v_ref, c_ref,
                 u_ref, d_ref, us_ref, ds_ref, b1_ref, b2_ref, hs_ref, g_ref,
                 fg_ref, rs_buf, z_buf, part, loads,
                 u_send, u_recv, d_send, d_recv, sums, known):
    at = place()
    ctx = lax.axis_index("ctx")
    halves = pl.ds(0, 1024), pl.ds(1024, 1024)
    sides = ((q_hbm, q_ref), (c_hbm, c_ref)), ((k_hbm, k_ref), (v_hbm, v_ref))

    def load(side, half):
        return [
            pltpu.make_async_copy(
                src.at[:, halves[half]], dst.at[:, halves[half]], loads.at[4 * side + 2 * half + n])
            for n, (src, dst) in enumerate(sides[side])
        ]

    small = [
        pltpu.make_async_copy(s_hbm, s_ref, loads.at[8]),
        pltpu.make_async_copy(h_hbm, h_ref, loads.at[9]),
    ]
    first = [small[0]] + load(0, 0) + load(1, 1)
    for copy in first:
        copy.start()
    barrier, greeted = greet(at)
    second = [small[1]] + load(0, 1) + load(1, 0)
    for copy in second:
        copy.start()
    for copy in first:
        copy.wait()
    keep_own = keep_of(s_ref, ctx * 128)
    keep_after = keep_of(s_ref, (ctx + 1) * 128)

    def dy_product(lanes):
        dy = c_ref[:, lanes].astype(F32) * q_ref[:, lanes].astype(F32)
        d_ref[0:128, lanes] = dy.astype(BF16)
        ds_ref[:, lanes] = (dy * keep_own).astype(BF16)

    def u_product(lanes):
        u = k_ref[:, lanes].astype(F32) * v_ref[:, lanes].astype(F32)
        u_ref[128:256, lanes] = u.astype(BF16)
        us_ref[:, lanes] = (u * keep_after).astype(BF16)

    def halo(by, lanes, n):
        if by == 1:
            return pltpu.make_async_remote_copy(
                us_ref.at[:, lanes], u_ref.at[pl.ds(0, 128), lanes],
                u_send.at[n], u_recv.at[n], beside(1), MESH)
        return pltpu.make_async_remote_copy(
            ds_ref.at[:, lanes], d_ref.at[pl.ds(128, 128), lanes],
            d_send.at[n], d_recv.at[n], beside(-1), MESH)

    def lanes_of(step, half):
        quarter, skip, count = STEPS[step]
        start = group_of(at, quarter) * 256 + 128 * skip + 1024 * half
        return pl.ds(pl.multiple_of(start, 128), 128 * count)

    def send(pair):
        only(-1, pair[0].start)
        only(1, pair[1].start)

    def receive(pair):
        only(1, pair[0].wait_recv)
        only(-1, pair[1].wait_recv)

    @pl.when(ctx == 0)
    def _():
        u_ref[0:128] = jnp.zeros((128, 2048), BF16)

    @pl.when(ctx == 63)
    def _():
        d_ref[128:256] = jnp.zeros((128, 2048), BF16)

    count = len(STEPS)
    soon = [
        (halo(-1, lanes_of(step, 0), step), halo(1, lanes_of(step, 1), step))
        for step in range(count)
    ]
    rest = halo(-1, halves[1], count), halo(1, halves[0], count)
    for step in range(count):
        dy_product(lanes_of(step, 0))
        u_product(lanes_of(step, 1))
        if step == 0:
            pl.semaphore_wait(barrier, greeted)
        send(soon[step])
        if step == 0:
            pass_on(at, known, 0)
            pass_on(at, known, 3)
    for copy in second:
        copy.wait()
    for j in range(4):
        dy_product(pl.ds(1024 + 256 * j, 256))
        u_product(pl.ds(256 * j, 256))
    learn(known, 0)
    pass_on(at, known, 1)
    learn(known, 3)
    pass_on(at, known, 4)
    build_bases(h_ref, hs_ref, b1_ref, b2_ref)
    learn(known, 1)
    pass_on(at, known, 2)
    learn(known, 4)
    pass_on(at, known, 5)
    lane = lax.broadcasted_iota(jnp.int32, (128, 128), 1)
    sub = lax.broadcasted_iota(jnp.int32, (128, 128), 0)
    turn = jnp.where(lane + sub == 128, 1.0, jnp.where(lane + sub == 0, 1.0, 0.0))

    def blocks_of(step):
        quarter, skip, blocks = STEPS[step]
        start = group_of(at, quarter) * 2 + skip
        slot = 4 * quarter + 2 * skip
        return [(start + i, slot + 2 * i) for i in range(blocks)]

    def sums_of(step):
        for block, slot in blocks_of(step):
            pair_sums(block, slot, u_ref, 128, d_ref, g_ref)
            pair_sums(8 + block, slot + 1, d_ref, 0, u_ref, g_ref)

    def diagonals_of(step):
        back = []
        for block, slot in blocks_of(step):
            fg_ref[block] = diagonals(slot, g_ref, 0)
            back.append(diagonals(slot + 1, g_ref, 1))
        back = jnp.dot(
            jnp.concatenate(back, axis=0), turn,
            precision=lax.Precision.HIGHEST, preferred_element_type=F32)
        for i, (block, _) in enumerate(blocks_of(step)):
            fg_ref[8 + block] = back[8 * i : 8 * i + 8]

    own = at["y"] * 4 + at["x"]
    mine = block_at(at["y"], at["x"])
    height = index_in(LINE, at)

    def hand_over(quarter):
        j = group_of(at, quarter)
        for dx in (2, 1, 3) if quarter == 3 else (2, 1, 3, 0):
            x = lax.rem(at["x"] + dx, 4)
            there = device({"y": j, "z": at["z"], "x": x, "core": at["core"]})
            pltpu.make_async_remote_copy(
                fg_ref.at[block_at(j, x)], rs_buf.at[own], sums.at[0], sums.at[1], there, MESH
            ).start()

    for step in range(count):
        receive(soon[step])
        if step > 0:
            diagonals_of(step - 1)
        sums_of(step)
        if step == 1:
            learn(known, 2)
            learn(known, 5)
            pass_on(at, known, 6)
        if 0 < step < 4:
            hand_over(step - 1)
    diagonals_of(count - 1)
    hand_over(3)
    rs_buf[own] = fg_ref[mine]
    send(rest)

    def outputs(i):
        conv_block(i, b1_ref, u_ref, (q_ref, c_ref), (z_ref, gq_ref))

    def gradients(i):
        conv_block(i, b2_ref, d_ref, (v_ref, k_ref), (gk_ref, gv_ref))

    def early(i, _):
        outputs(8 + i)
        gradients(i)
        return 0

    def later(i, _):
        outputs(i)
        gradients(8 + i)
        return 0

    lax.fori_loop(0, SPLIT[0], early, 0)
    wait_all(rs_buf, sums.at[1])
    part[0] = tree_sum(rs_buf)
    learn(known, 6)
    send_all(LINE, at, lambda p: part.at[0], z_buf, sums.at[2], sums.at[3])
    z_buf[height] = part[0]
    lax.fori_loop(SPLIT[0], 8, early, 0)

    receive(rest)
    lax.fori_loop(0, SPLIT[1], later, 0)
    wait_all(z_buf, sums.at[3])
    part[1] = tree_sum(z_buf)
    for offset in others(PLANE):
        there = device(shifted(PLANE, at, offset))
        pltpu.make_async_remote_copy(
            part.at[1], put_ref.at[mine], sums.at[4], sums.at[5], there, MESH).start()
    put_ref[mine] = part[1]
    lax.fori_loop(SPLIT[1], 8, later, 0)

    for pair in soon + [rest]:
        only(-1, pair[0].wait_send)
        only(1, pair[1].wait_send)
    wait_all(rs_buf, sums.at[0])
    wait_all(z_buf, sums.at[2])
    wait_all(put_ref, sums.at[4])
    wait_all(put_ref, sums.at[5])


SPLIT = (3, 3)


def whole(h, starts, q, k, v, c):
    sd = jax.ShapeDtypeStruct
    vmem = pl.BlockSpec(memory_space=pltpu.VMEM)
    hbm = pl.BlockSpec(memory_space=pl.ANY)
    act = pltpu.VMEM((128, 2048), BF16)
    two = pltpu.VMEM((256, 2048), BF16)
    base = pltpu.VMEM((2048, 256), BF16)
    dma = pltpu.SemaphoreType.DMA
    return pl.pallas_call(
        whole_kernel,
        out_shape=[pltpu.VMEM((128, 2048), BF16)] * 4 + [pltpu.VMEM((16, 8, 128), F32)],
        in_specs=[hbm] * 6,
        out_specs=[vmem] * 5,
        scratch_shapes=[
            pltpu.VMEM((128, 128), BF16), pltpu.SMEM((1, 17), jnp.int32), act, act, act, act,
            two, two, act, act, base, base,
            pltpu.VMEM((2, 128, 128), F32), pltpu.VMEM((16, 128, 256), F32),
            pltpu.VMEM((16, 8, 128), F32), pltpu.VMEM((16, 8, 128), F32),
            pltpu.VMEM((16, 8, 128), F32), pltpu.VMEM((2, 8, 128), F32),
            dma((10,)), dma((6,)), dma((6,)), dma((6,)), dma((6,)), dma((6,)),
            pltpu.SemaphoreType.REGULAR((len(ROUNDS),)),
        ],
        compiler_params=pltpu.CompilerParams(
            collective_id=0, has_side_effects=True, vmem_limit_bytes=VMEM_LIMIT),
        name="whole_operator",
    )(*[pltpu.with_memory_space_constraint(x, pltpu.HBM) for x in (h, starts, q, k, v, c)])


VMEM_LIMIT = 32 * 1024 * 1024


def finish_kernel(*refs):
    sems = refs[10]
    copies = [pltpu.make_async_copy(refs[i], refs[5 + i], sems.at[i]) for i in range(5)]
    for copy in copies:
        copy.start()
    for copy in copies:
        copy.wait()


def finish(arrays):
    hbm = pl.BlockSpec(memory_space=pl.ANY)
    return pl.pallas_call(
        finish_kernel,
        out_shape=[pltpu.HBM(a.shape, a.dtype) for a in arrays],
        in_specs=[hbm] * 5,
        out_specs=[hbm] * 5,
        scratch_shapes=[pltpu.SemaphoreType.DMA((5,))],
        compiler_params=pltpu.CompilerParams(vmem_limit_bytes=1024 * 1024),
        name="finish",
    )(*[pltpu.with_memory_space_constraint(a, pltpu.VMEM) for a in arrays])


def per_device(gate_in, key_in, value_in, cotangent, doc_starts, filters):
    z, gq, gk, gv, put = finish(whole(
        filters, doc_starts, gate_in[0], key_in[0], value_in[0], cotangent[0]))
    return z[None], gq[None], gk[None], gv[None], put.reshape(128, 128)


def solution(mesh):
    rows = P("dp", "ctx", None)
    return jax.shard_map(
        per_device,
        mesh=mesh,
        in_specs=(rows, rows, rows, rows, P("dp", None), P()),
        out_specs=(rows, rows, rows, rows, P()),
        check_vma=False,
    )
```

```python
import itertools

import jax
import jax.numpy as jnp
from jax import lax
from jax.experimental import pallas as pl
from jax.experimental.pallas import tpu as pltpu
from jax.sharding import PartitionSpec as P

F32, BF16 = jnp.float32, jnp.bfloat16
MESH = pl.DeviceIdType.MESH
NT = (((1,), (1,)), ((), ()))


def build_bases(h_ref, hs_ref, b1_ref, b2_ref):
    lane = lax.broadcasted_iota(jnp.int32, (128, 128), 1)
    sub = lax.broadcasted_iota(jnp.int32, (128, 128), 0)
    flip = (lane + sub == 127).astype(BF16)
    h = h_ref[...]
    hs_ref[0] = h.astype(F32)
    hs_ref[1] = jnp.dot(h, flip, preferred_element_type=F32)
    r = lax.broadcasted_iota(jnp.int32, (16, 128), 0)
    m = lax.broadcasted_iota(jnp.int32, (16, 128), 1)

    def step(i, _):
        for j in range(8):
            f = i * 8 + j
            rows = pl.ds(pl.multiple_of(f * 16, 16), 16)
            fwd = jnp.broadcast_to(hs_ref[0, pl.ds(f, 1), :], (16, 128))
            rev = jnp.broadcast_to(hs_ref[1, pl.ds(f, 1), :], (16, 128))
            fwd = pltpu.roll(fwd, 0, 1, stride=1, stride_axis=0)
            rev = pltpu.roll(rev, 1, 1, stride=1, stride_axis=0)
            b2_ref[rows, 0:128] = jnp.where(m >= r, fwd, 0.0).astype(BF16)
            b2_ref[rows, 128:256] = jnp.where(m < r, fwd, 0.0).astype(BF16)
            b1_ref[rows, 0:128] = jnp.where(m >= r + 1, rev, 0.0).astype(BF16)
            b1_ref[rows, 128:256] = jnp.where(m < r + 1, rev, 0.0).astype(BF16)
        return 0

    lax.fori_loop(0, 16, step, 0)


def pick(full, half, group):
    lanes = slice(128 * half, 128 * half + 128)
    out = full[112:128, lanes]
    for g in range(6, -1, -1):
        out = jnp.where(group == g, full[16 * g : 16 * g + 16, lanes], out)
    return out


def slab(ref, a, blk):
    return jnp.concatenate(
        [ref[16 * a : 16 * a + 144, blk], ref[16 * a + 16 : 16 * a + 160, blk]], axis=1
    )


def block_of(i):
    return pl.ds(pl.multiple_of(i * 128, 128), 128)


def lane_group():
    return lax.broadcasted_iota(jnp.int32, (16, 128), 1) // 16


def conv_block(i, bases, source, gates, results):
    blk = block_of(i)
    group = lane_group()
    lhs = bases[blk, 0:144]
    for a in range(0, 8, 2):
        full = jnp.dot(lhs, slab(source, a, blk), preferred_element_type=F32)
        for half in range(2):
            rows = slice(16 * (a + half), 16 * (a + half) + 16)
            value = pick(full, half, group)
            for gate, result in zip(gates, results):
                result[rows, blk] = (gate[rows, blk].astype(F32) * value).astype(BF16)


def pair_sums(i, slot, rows_ref, first, slab_ref, g_ref):
    blk = block_of(i)
    group = lane_group()
    total = jnp.zeros((128, 144), F32)
    for a in range(0, 8, 2):
        pair = []
        for half in range(2):
            start = first + 16 * (a + half)
            rows = rows_ref[start : start + 16, blk]
            spread = [jnp.where(group == g, rows, jnp.zeros_like(rows)) for g in range(8)]
            pair.append(jnp.concatenate(spread, axis=0))
        total = total + lax.dot_general(
            jnp.concatenate(pair, axis=1), slab(slab_ref, a, blk), NT, preferred_element_type=F32
        )
    g_ref[slot, :, 0:144] = total


def diagonals(slot, g_ref, shift):
    lane = lax.broadcasted_iota(jnp.int32, (128, 128), 1)
    r = lax.broadcasted_iota(jnp.int32, (128, 128), 0) % 16
    both = jnp.where(lane < r + shift, g_ref[slot, :, 128:256], g_ref[slot, :, 0:128])
    parts = [
        both[16 * f : 16 * f + 8] + pltpu.roll(both[16 * f + 8 : 16 * f + 16], 120, 1)
        for f in range(8)
    ]
    sub = lax.broadcasted_iota(jnp.int32, (8, 128), 0)
    for step in (4, 2, 1):
        low = sub % (2 * step) < step
        merged = []
        for f in range(step):
            one, two = parts[f], parts[f + step]
            first = jnp.where(low, one, pltpu.roll(two, step, 0))
            second = jnp.where(low, pltpu.roll(one, 8 - step, 0), two)
            merged.append(first + pltpu.roll(second, 128 - step, 1))
        parts = merged
    return parts[0]


STEPS = ((0, 0, 2), (1, 0, 2), (2, 0, 2), (3, 0, 1), (3, 1, 1))
SIZES = {"y": 4, "z": 8, "x": 4, "core": 2}
PLANE, LINE = ("y", "x"), ("z", "core")


def place():
    ctx = lax.axis_index("ctx")
    return {
        "y": lax.axis_index("dp"),
        "z": ctx // 8,
        "x": lax.rem(ctx // 2, 4),
        "core": lax.rem(ctx, 2),
    }


def device(at):
    return {"dp": at["y"], "ctx": (at["z"] * 4 + at["x"]) * 2 + at["core"]}


def index_in(axes, at):
    index = 0
    for axis in axes:
        index = index * SIZES[axis] + at[axis]
    return index


def others(axes):
    def hops(offset):
        return sum(
            0.1 * d if axis == "core" else min(d, SIZES[axis] - d)
            for axis, d in zip(axes, offset)
        )

    every = itertools.product(*[range(SIZES[axis]) for axis in axes])
    return sorted([o for o in every if any(o)], key=lambda o: -hops(o))


def shifted(axes, at, offset):
    at = dict(at)
    for axis, d in zip(axes, offset):
        if d:
            at[axis] = lax.rem(at[axis] + d, SIZES[axis])
    return at


def beside(by):
    return {"ctx": lax.rem(lax.axis_index("ctx") + 64 + by, 64)}


NEAR = (("x", 1), ("x", 3), ("y", 1), ("y", 3), ("z", 1), ("z", 7), ("core", 1))


def only(by, act):
    ctx = lax.axis_index("ctx")
    pl.when(ctx < 63 if by == 1 else ctx > 0)(act)


def greet(at):
    barrier = pltpu.get_barrier_semaphore()
    for by in (1, -1):
        only(by, lambda: pl.semaphore_signal(
            barrier, 1, device_id=beside(by), device_id_type=MESH))
    for axis, by in NEAR:
        there = device(shifted((axis,), at, (by,)))
        pl.semaphore_signal(barrier, 1, device_id=there, device_id_type=MESH)
    ctx = lax.axis_index("ctx")
    at_end = jnp.logical_or(ctx == 0, ctx == 63)
    return barrier, jnp.where(at_end, 1, 2) + len(NEAR)


ROUNDS = (
    (("x", 3),),
    (("y", 1), ("y", 3)),
    (("y", 3),),
    (("z", 1), ("z", 7)),
    (("z", 1), ("z", 7)),
    (("z", 1), ("z", 7)),
    (("z", 7),),
)


def pass_on(at, known, n):
    for axis, by in ROUNDS[n]:
        there = device(shifted((axis,), at, (by,)))
        pl.semaphore_signal(known.at[n], 1, device_id=there, device_id_type=MESH)


def learn(known, n):
    pl.semaphore_wait(known.at[n], len(ROUNDS[n]))


def group_of(at, step):
    return lax.rem(at["y"] + (2, 1, 3, 0)[step], 4)


def block_at(y, x):
    return 2 * y + x + jnp.where(x >= 2, 6, 0)


def send_all(axes, at, src_of, dst, send, recv):
    own = index_in(axes, at)
    for offset in others(axes):
        there = shifted(axes, at, offset)
        pltpu.make_async_remote_copy(
            src_of(index_in(axes, there)), dst.at[own], send, recv, device(there), MESH).start()


def wait_all(dst, sem):
    most = dst.at[pl.ds(0, dst.shape[0] - 1)]
    pltpu.make_async_copy(most, most, sem).wait()


def tree_sum(ref):
    terms = [ref[i] for i in range(ref.shape[0])]
    while len(terms) > 1:
        terms = [sum(terms[i : i + 2]) for i in range(0, len(terms), 2)]
    return terms[0]


def keep_of(starts_ref, position):
    hit = starts_ref[0, 0] == position
    for i in range(1, 17):
        hit = jnp.logical_or(hit, starts_ref[0, i] == position)
    return jnp.where(hit, 0.0, 1.0)


def whole_kernel(h_hbm, s_hbm, q_hbm, k_hbm, v_hbm, c_hbm,
                 z_ref, gq_ref, gk_ref, gv_ref, put_ref,
                 h_ref, s_ref, q_ref, k_ref, v_ref, c_ref,
                 u_ref, d_ref, us_ref, ds_ref, b1_ref, b2_ref, hs_ref, g_ref,
                 fg_ref, rs_buf, z_buf, part, loads,
                 u_send, u_recv, d_send, d_recv, sums, known):
    at = place()
    ctx = lax.axis_index("ctx")
    halves = pl.ds(0, 1024), pl.ds(1024, 1024)
    sides = ((q_hbm, q_ref), (c_hbm, c_ref)), ((k_hbm, k_ref), (v_hbm, v_ref))

    def load(side, half):
        return [
            pltpu.make_async_copy(
                src.at[:, halves[half]], dst.at[:, halves[half]], loads.at[4 * side + 2 * half + n])
            for n, (src, dst) in enumerate(sides[side])
        ]

    small = [
        pltpu.make_async_copy(s_hbm, s_ref, loads.at[8]),
        pltpu.make_async_copy(h_hbm, h_ref, loads.at[9]),
    ]
    first = [small[0]] + load(0, 0) + load(1, 1)
    for copy in first:
        copy.start()
    barrier, greeted = greet(at)
    second = [small[1]] + load(0, 1) + load(1, 0)
    for copy in second:
        copy.start()
    for copy in first:
        copy.wait()
    keep_own = keep_of(s_ref, ctx * 128)
    keep_after = keep_of(s_ref, (ctx + 1) * 128)

    def dy_product(lanes):
        dy = c_ref[:, lanes].astype(F32) * q_ref[:, lanes].astype(F32)
        d_ref[0:128, lanes] = dy.astype(BF16)
        ds_ref[:, lanes] = (dy * keep_own).astype(BF16)

    def u_product(lanes):
        u = k_ref[:, lanes].astype(F32) * v_ref[:, lanes].astype(F32)
        u_ref[128:256, lanes] = u.astype(BF16)
        us_ref[:, lanes] = (u * keep_after).astype(BF16)

    def halo(by, lanes, n):
        if by == 1:
            return pltpu.make_async_remote_copy(
                us_ref.at[:, lanes], u_ref.at[pl.ds(0, 128), lanes],
                u_send.at[n], u_recv.at[n], beside(1), MESH)
        return pltpu.make_async_remote_copy(
            ds_ref.at[:, lanes], d_ref.at[pl.ds(128, 128), lanes],
            d_send.at[n], d_recv.at[n], beside(-1), MESH)

    def lanes_of(step, half):
        quarter, skip, count = STEPS[step]
        start = group_of(at, quarter) * 256 + 128 * skip + 1024 * half
        return pl.ds(pl.multiple_of(start, 128), 128 * count)

    def send(pair):
        only(-1, pair[0].start)
        only(1, pair[1].start)

    def receive(pair):
        only(1, pair[0].wait_recv)
        only(-1, pair[1].wait_recv)

    @pl.when(ctx == 0)
    def _():
        u_ref[0:128] = jnp.zeros((128, 2048), BF16)

    @pl.when(ctx == 63)
    def _():
        d_ref[128:256] = jnp.zeros((128, 2048), BF16)

    count = len(STEPS)
    soon = [
        (halo(-1, lanes_of(step, 0), step), halo(1, lanes_of(step, 1), step))
        for step in range(count)
    ]
    rest = halo(-1, halves[1], count), halo(1, halves[0], count)
    for step in range(count):
        dy_product(lanes_of(step, 0))
        u_product(lanes_of(step, 1))
        if step == 0:
            pl.semaphore_wait(barrier, greeted)
        send(soon[step])
        if step == 0:
            pass_on(at, known, 0)
            pass_on(at, known, 3)
    for copy in second:
        copy.wait()
    for j in range(4):
        dy_product(pl.ds(1024 + 256 * j, 256))
        u_product(pl.ds(256 * j, 256))
    learn(known, 0)
    pass_on(at, known, 1)
    learn(known, 3)
    pass_on(at, known, 4)
    build_bases(h_ref, hs_ref, b1_ref, b2_ref)
    learn(known, 1)
    pass_on(at, known, 2)
    learn(known, 4)
    pass_on(at, known, 5)
    def blocks_of(step):
        quarter, skip, blocks = STEPS[step]
        start = group_of(at, quarter) * 2 + skip
        slot = 4 * quarter + 2 * skip
        return [(start + i, slot + 2 * i) for i in range(blocks)]

    def sums_of(step):
        for block, slot in blocks_of(step):
            pair_sums(block, slot, u_ref, 128, d_ref, g_ref)
            pair_sums(8 + block, slot + 1, d_ref, 0, u_ref, g_ref)

    def diagonals_of(step):
        for block, slot in blocks_of(step):
            fg_ref[block] = diagonals(slot, g_ref, 0)
            fg_ref[8 + block] = diagonals(slot + 1, g_ref, 1)

    own = at["y"] * 4 + at["x"]
    mine = block_at(at["y"], at["x"])
    height = index_in(LINE, at)

    def hand_over(quarter):
        j = group_of(at, quarter)
        for dx in (2, 1, 3) if quarter == 3 else (2, 1, 3, 0):
            x = lax.rem(at["x"] + dx, 4)
            there = device({"y": j, "z": at["z"], "x": x, "core": at["core"]})
            pltpu.make_async_remote_copy(
                fg_ref.at[block_at(j, x)], rs_buf.at[own], sums.at[0], sums.at[1], there, MESH
            ).start()

    for step in range(count):
        receive(soon[step])
        if step > 0:
            diagonals_of(step - 1)
        sums_of(step)
        if step == 1:
            learn(known, 2)
            learn(known, 5)
            pass_on(at, known, 6)
        if 0 < step < 4:
            hand_over(step - 1)
    diagonals_of(count - 1)
    hand_over(3)
    rs_buf[own] = fg_ref[mine]
    send(rest)

    def outputs(i):
        conv_block(i, b1_ref, u_ref, (q_ref, c_ref), (z_ref, gq_ref))

    def gradients(i):
        conv_block(i, b2_ref, d_ref, (v_ref, k_ref), (gk_ref, gv_ref))

    def early(i, _):
        outputs(8 + i)
        gradients(i)
        return 0

    def later(i, _):
        outputs(i)
        gradients(8 + i)
        return 0

    lax.fori_loop(0, SPLIT[0], early, 0)
    wait_all(rs_buf, sums.at[1])
    part[0] = tree_sum(rs_buf)
    learn(known, 6)
    send_all(LINE, at, lambda p: part.at[0], z_buf, sums.at[2], sums.at[3])
    z_buf[height] = part[0]
    lax.fori_loop(SPLIT[0], 8, early, 0)

    receive(rest)
    lax.fori_loop(0, SPLIT[1], later, 0)
    wait_all(z_buf, sums.at[3])
    part[1] = tree_sum(z_buf)
    for offset in others(PLANE):
        there = device(shifted(PLANE, at, offset))
        pltpu.make_async_remote_copy(
            part.at[1], put_ref.at[mine], sums.at[4], sums.at[5], there, MESH).start()
    put_ref[mine] = part[1]
    lax.fori_loop(SPLIT[1], 8, later, 0)

    for pair in soon + [rest]:
        only(-1, pair[0].wait_send)
        only(1, pair[1].wait_send)
    wait_all(rs_buf, sums.at[0])
    wait_all(z_buf, sums.at[2])
    wait_all(put_ref, sums.at[4])
    wait_all(put_ref, sums.at[5])


SPLIT = (3, 3)


def whole(h, starts, q, k, v, c):
    sd = jax.ShapeDtypeStruct
    vmem = pl.BlockSpec(memory_space=pltpu.VMEM)
    hbm = pl.BlockSpec(memory_space=pl.ANY)
    act = pltpu.VMEM((128, 2048), BF16)
    two = pltpu.VMEM((256, 2048), BF16)
    base = pltpu.VMEM((2048, 256), BF16)
    dma = pltpu.SemaphoreType.DMA
    return pl.pallas_call(
        whole_kernel,
        out_shape=[pltpu.VMEM((128, 2048), BF16)] * 4 + [pltpu.VMEM((16, 8, 128), F32)],
        in_specs=[hbm] * 6,
        out_specs=[vmem] * 5,
        scratch_shapes=[
            pltpu.VMEM((128, 128), BF16), pltpu.SMEM((1, 17), jnp.int32), act, act, act, act,
            two, two, act, act, base, base,
            pltpu.VMEM((2, 128, 128), F32), pltpu.VMEM((16, 128, 256), F32),
            pltpu.VMEM((16, 8, 128), F32), pltpu.VMEM((16, 8, 128), F32),
            pltpu.VMEM((16, 8, 128), F32), pltpu.VMEM((2, 8, 128), F32),
            dma((10,)), dma((6,)), dma((6,)), dma((6,)), dma((6,)), dma((6,)),
            pltpu.SemaphoreType.REGULAR((len(ROUNDS),)),
        ],
        compiler_params=pltpu.CompilerParams(
            collective_id=0, has_side_effects=True, vmem_limit_bytes=VMEM_LIMIT),
        name="whole_operator",
    )(*[pltpu.with_memory_space_constraint(x, pltpu.HBM) for x in (h, starts, q, k, v, c)])


VMEM_LIMIT = 32 * 1024 * 1024


def finish_kernel(*refs):
    put_ref, put_hbm, sems, turned = refs[4], refs[9], refs[10], refs[11]
    copies = [pltpu.make_async_copy(refs[i], refs[5 + i], sems.at[i]) for i in range(4)]
    for copy in copies:
        copy.start()
    lane = lax.broadcasted_iota(jnp.int32, (128, 128), 1)
    sub = lax.broadcasted_iota(jnp.int32, (128, 128), 0)
    turn = jnp.where(lane + sub == 128, 1.0, jnp.where(lane + sub == 0, 1.0, 0.0))
    turned[0:8] = put_ref[0:8]
    turned[8:16] = jnp.dot(
        put_ref[8:16].reshape(64, 128), turn,
        precision=lax.Precision.HIGHEST, preferred_element_type=F32).reshape(8, 8, 128)
    last = pltpu.make_async_copy(turned, put_hbm, sems.at[4])
    last.start()
    for copy in copies + [last]:
        copy.wait()


def finish(arrays):
    hbm = pl.BlockSpec(memory_space=pl.ANY)
    return pl.pallas_call(
        finish_kernel,
        out_shape=[pltpu.HBM(a.shape, a.dtype) for a in arrays],
        in_specs=[hbm] * 4 + [pl.BlockSpec(memory_space=pltpu.VMEM)],
        out_specs=[hbm] * 5,
        scratch_shapes=[pltpu.SemaphoreType.DMA((5,)), pltpu.VMEM((16, 8, 128), F32)],
        compiler_params=pltpu.CompilerParams(vmem_limit_bytes=1024 * 1024),
        name="finish",
    )(*[pltpu.with_memory_space_constraint(a, pltpu.VMEM) for a in arrays])


def per_device(gate_in, key_in, value_in, cotangent, doc_starts, filters):
    z, gq, gk, gv, put = finish(whole(
        filters, doc_starts, gate_in[0], key_in[0], value_in[0], cotangent[0]))
    return z[None], gq[None], gk[None], gv[None], put.reshape(128, 128)


def solution(mesh):
    rows = P("dp", "ctx", None)
    return jax.shard_map(
        per_device,
        mesh=mesh,
        in_specs=(rows, rows, rows, rows, P("dp", None), P()),
        out_specs=(rows, rows, rows, rows, P()),
        check_vma=False,
    )
```
